512 devices in a mesh: rep: 8 (over z_lo), fsdp: 64 (over z_hi, x, y, core).
Axes of the slice: x: 4, y: 4, z: 16 (z_hi: 2, z_lo: 8; z = z_hi * 8 + z_lo), core: 2. Of those that a mesh axis runs over, the one named last changes fastest.
Arguments:
- base_weights: bfloat16 [4096, 8192], P('fsdp'), may hold values from -6 to 6
- local_weights: bfloat16 [8, 4096, 8192], P('rep', 'fsdp'), may hold values from -6 to 6
- outer_params: float32 [4096, 8192], P('rep', 'fsdp'), may hold values from -6 to 6
- momentum: float32 [4096, 8192], P('rep', 'fsdp'), may hold values from -4 to 4
Outputs:
- new_outer: float32 [4096, 8192], P('rep', 'fsdp')
- new_momentum: float32 [4096, 8192], P('rep', 'fsdp')
- new_weights: bfloat16 [4096, 8192], P('fsdp')
The draws below stay inside these ranges and needn't reach their ends.
All inputs are finite; a program needn't handle non-finite values.
Results may differ from the reference program's by a relative error of at most 0.012.
Values may be sent and summed in bfloat16 or wider, within the bound.
A program may use at most 64 MiB of HBM per device.

```python
import jax
import jax.numpy as jnp
from jax import lax

D = 8192
BLOCK = 128
ROWS = 4096
REPLICAS = 8


def block_levels(rng, dims, split, least, high):
    loudness = 1.0
    for position, shards_of in split:
        draws = jax.random.uniform(jax.random.fold_in(jax.random.fold_in(rng, 6), position), (shards_of,), jnp.float32, least / len(split), high / len(split))
        loudness = loudness * jnp.repeat(jnp.exp(draws), dims[position] // shards_of).reshape((-1,) + (1,) * (len(dims) - 1 - position))
    return loudness


def bell_draw(stream_key, extent, width, limit, split=(), kind=jnp.bfloat16):
    level = block_levels(stream_key, extent, split, -0.22, 0.18) if split else 1.0
    array = jax.random.normal(stream_key, extent, jnp.float32) * width * level
    return jnp.minimum(jnp.maximum(array, -limit), limit).astype(kind)


def setup_inputs(seed: int = 0) -> dict:
    key_of = jax.random.split(jax.random.key(seed), 5)
    return {
        "base_weights": bell_draw(key_of[0], (ROWS, D), 1.0, 6.0, ((0, 64),)),
        "local_weights": bell_draw(key_of[1], (REPLICAS, ROWS, D), 1.0, 6.0, ((0, 8), (1, 64))),
        "outer_params": bell_draw(key_of[2], (ROWS, D), 1.0, 6.0, ((0, 8), (1, 64)), jnp.float32),
        "momentum": bell_draw(key_of[3], (ROWS, D), 0.5, 4.0, ((0, 8), (1, 64)), jnp.float32),
    }


LEVEL_LIMIT = 448.0
EPSILON = 1e-6
OUTER_RATE = 0.7
MOMENTUM_DECAY = 0.9


def quantize(pseudo):
    blocks = pseudo.reshape(ROWS, D // BLOCK, BLOCK)
    largest = jnp.max(jnp.abs(blocks), axis=2)
    scales = ((largest + EPSILON) / LEVEL_LIMIT).astype(jnp.bfloat16)
    levels = (blocks / scales.astype(jnp.float32)[:, :, None]).astype(jnp.bfloat16)
    return levels, scales


def reference(base_weights, local_weights, outer_params, momentum):
    base_wide = base_weights.astype(jnp.float32)

    def add_replica(summed, local_shard):
        pseudo = base_wide - local_shard.astype(jnp.float32)
        levels, scales = quantize(pseudo)
        return summed + levels.astype(jnp.float32) * scales.astype(jnp.float32)[:, :, None], None

    start_sum = jnp.zeros((ROWS, D // BLOCK, BLOCK), jnp.float32)
    summed, unused = lax.scan(add_replica, start_sum, local_weights)
    average = summed.reshape(ROWS, D) / REPLICAS
    new_momentum = MOMENTUM_DECAY * momentum + average
    new_outer = outer_params - OUTER_RATE * (average + MOMENTUM_DECAY * new_momentum)
    return new_outer, new_momentum, new_outer.astype(jnp.bfloat16)
```

```python
import functools

import jax
import jax.numpy as jnp
from jax import lax
from jax.experimental import pallas as pl
from jax.experimental.pallas import tpu as pltpu
from jax.sharding import Mesh
from jax.sharding import PartitionSpec as P

BLOCK = 128
LEVEL_LIMIT = 448.0
EPSILON = 1e-06
OUTER_RATE = 0.7
MOMENTUM_DECAY = 0.9
MESH = pl.DeviceIdType.MESH

FROM_MOMENTUM = OUTER_RATE * MOMENTUM_DECAY * MOMENTUM_DECAY
FROM_AVERAGE = OUTER_RATE * (1.0 + MOMENTUM_DECAY)

PARTS = 4
LAG = 4
GATHER_PARTS = 4


def kernel(n, base_hbm, local_hbm, outer_hbm, momentum_hbm, new_outer_hbm, new_momentum_hbm, weights_hbm,
           base, local, outer, momentum, new_outer, new_momentum,
           own, sums, from_left, from_right, gathered, prior_out, prior_in, total_out, total_in,
           in_sem, out_sem, right_send, right_recv, left_send, left_recv,
           prior_send, prior_recv, total_send, total_recv, ag_right_send, ag_left_send, ag_recv, weights_sem):
    a, b, l = lax.axis_index("rep"), lax.axis_index("hi"), lax.axis_index("lo")
    last = n - 1
    per_chunk = own.shape[0]
    wide = per_chunk // PARTS
    mirrored = a == b

    ins = [
        pltpu.make_async_copy(src, dst, in_sem.at[k])
        for k, (src, dst) in enumerate(
            ((outer_hbm, outer), (momentum_hbm, momentum), (base_hbm, base), (local_hbm, local))
        )
    ]
    for copy in ins:
        copy.start()

    barrier = pltpu.get_barrier_semaphore()

    @pl.when(a > 0)
    def _():
        pl.semaphore_signal(barrier, inc=1, device_id={"rep": a - 1}, device_id_type=MESH)

    @pl.when(a < last)
    def _():
        pl.semaphore_signal(barrier, inc=1, device_id={"rep": a + 1}, device_id_type=MESH)

    for j in range(n):
        @pl.when(jnp.logical_not(mirrored & (l == j)))
        def _():
            pl.semaphore_signal(barrier, inc=1, device_id=(b, a, j), device_id_type=MESH)

    greeted = n + 2 - (a == 0).astype(jnp.int32) - (a == last).astype(jnp.int32) - mirrored.astype(jnp.int32)

    def exchange(j, src, dst, send_sem, recv_sem):
        return pltpu.make_async_remote_copy(
            src_ref=src.at[j], dst_ref=dst.at[l], send_sem=send_sem.at[j], recv_sem=recv_sem.at[l],
            device_id=(b, a, j), device_id_type=MESH)

    def keep(j, src, dst, recv_sem):
        return pltpu.make_async_copy(src.at[j], dst.at[j], recv_sem.at[j])

    def start_exchange(j, src, dst, send_sem, recv_sem):
        mine = mirrored & (l == j)

        @pl.when(mine)
        def _():
            keep(j, src, dst, recv_sem).start()

        @pl.when(jnp.logical_not(mine))
        def _():
            exchange(j, src, dst, send_sem, recv_sem).start()

    def wait_exchange(j, src, dst, send_sem, recv_sem):
        mine = mirrored & (l == j)

        @pl.when(mine)
        def _():
            keep(j, src, dst, recv_sem).wait()

        @pl.when(jnp.logical_not(mine))
        def _():
            pltpu.make_async_remote_copy(
                src_ref=src.at[j], dst_ref=dst.at[j], send_sem=send_sem.at[j], recv_sem=recv_sem.at[j],
                device_id=(b, a, j), device_id_type=MESH).wait_recv()

    def wait_sent(j, src, dst, send_sem, recv_sem):
        @pl.when(jnp.logical_not(mirrored & (l == j)))
        def _():
            exchange(j, src, dst, send_sem, recv_sem).wait_send()

    def dequantized(block):
        columns = pl.ds(pl.multiple_of(block * BLOCK, BLOCK), BLOCK)
        pseudo = base[:, columns].astype(jnp.float32) - local[:, columns].astype(jnp.float32)
        largest = jnp.max(jnp.abs(pseudo), axis=1, keepdims=True)
        scale = ((largest + EPSILON) / LEVEL_LIMIT).astype(jnp.bfloat16).astype(jnp.float32)
        levels = (pseudo / scale).astype(jnp.bfloat16).astype(jnp.float32)
        return levels * scale

    ins[0].wait()
    ins[1].wait()
    rows = prior_out.shape[1]
    for j in range(n):
        part = pl.ds(j * rows, rows)
        prior_out[j] = (outer[part, :] - FROM_MOMENTUM * momentum[part, :]).astype(jnp.bfloat16)
    pl.semaphore_wait(barrier, greeted)
    prior = (prior_out, prior_in, prior_send, prior_recv)
    for j in range(n):
        start_exchange(j, *prior)
    ins[2].wait()
    ins[3].wait()

    def passed_on(arrived, send_sem, recv_sem, block, to):
        return pltpu.make_async_remote_copy(
            src_ref=sums.at[pl.ds(block, wide)], dst_ref=arrived.at[pl.ds(block, wide)],
            send_sem=send_sem.at[block // wide], recv_sem=recv_sem.at[block // wide],
            device_id={"rep": to}, device_id_type=MESH)

    def pass_on(has_input, arrived, send_sem, recv_sem, block, to):
        copy = passed_on(arrived, send_sem, recv_sem, block, to)
        for k in range(wide):
            own[k] = dequantized(block + k)

        @pl.when(has_input)
        def _():
            copy.wait_recv()
            for k in range(wide):
                sums[block + k] = (own[k] + arrived[block + k].astype(jnp.float32)).astype(jnp.bfloat16)

        @pl.when(jnp.logical_not(has_input))
        def _():
            for k in range(wide):
                sums[block + k] = own[k].astype(jnp.bfloat16)

        copy.start()

    def right_block(u):
        return ((last - u // PARTS) * PARTS + u % PARTS) * wide

    def left_block(v):
        return v * wide

    right_to, left_to = jnp.minimum(a + 1, last), jnp.maximum(a - 1, 0)
    right = (from_left, right_send, right_recv)
    left = (from_right, left_send, left_recv)
    right_count, left_count = (last - a) * PARTS, a * PARTS

    def step(t, carry):
        u, v = t - a * LAG, t - (last - a) * LAG

        @pl.when((u >= 0) & (u < right_count))
        def _():
            pass_on(a > 0, *right, right_block(u), right_to)

        @pl.when((v >= 0) & (v < left_count))
        def _():
            pass_on(a < last, *left, left_block(v), left_to)

        return carry

    lax.fori_loop(0, last * max(LAG, PARTS), step, None)

    for j in range(n):
        own[j] = dequantized(a * per_chunk + j)
    for j in range(n):
        wait_exchange(j, *prior)
    totals = (total_out, total_in, total_send, total_recv)
    gather_wide = per_chunk // GATHER_PARTS

    def gather_copy(block, send_sem, to):
        return pltpu.make_async_remote_copy(
            src_ref=gathered.at[pl.ds(block, gather_wide)], dst_ref=gathered.at[pl.ds(block, gather_wide)],
            send_sem=send_sem.at[block // gather_wide], recv_sem=ag_recv.at[block // gather_wide],
            device_id={"rep": to}, device_id_type=MESH)

    def write_out(block):
        columns = pl.ds(pl.multiple_of(block * BLOCK, BLOCK), BLOCK)
        return pltpu.make_async_copy(gathered.at[block], weights_hbm.at[:, columns], weights_sem.at[block])

    def hand_on(block):
        @pl.when(a < last)
        def _():
            gather_copy(block, ag_right_send, right_to).start()

        @pl.when(a > 0)
        def _():
            gather_copy(block, ag_left_send, left_to).start()

    for q in range(PARTS):
        block = a * per_chunk + q * wide

        @pl.when(a > 0)
        def _():
            passed_on(from_left, right_send, right_recv, block, right_to).wait_recv()
            for k in range(wide):
                own[q * wide + k] += from_left[block + k].astype(jnp.float32)

        @pl.when(a < last)
        def _():
            passed_on(from_right, left_send, left_recv, block, left_to).wait_recv()
            for k in range(wide):
                own[q * wide + k] += from_right[block + k].astype(jnp.float32)

        for k in range(wide):
            j = q * wide + k
            total = own[j]
            total_out[j] = total.astype(jnp.bfloat16)
            gathered[block + k] = (
                prior_in[j].astype(jnp.float32) - (FROM_AVERAGE / n) * total).astype(jnp.bfloat16)
        hand_on(block)
        for k in range(wide):
            start_exchange(q * wide + k, *totals)
    for j in range(n):
        write_out(a * per_chunk + j).start()

    for s in range(1, n):
        for q in range(GATHER_PARTS):
            @pl.when(a - s >= 0)
            def _():
                block = (a - s) * per_chunk + q * gather_wide
                gather_copy(block, ag_right_send, right_to).wait_recv()

                @pl.when(a < last)
                def _():
                    gather_copy(block, ag_right_send, right_to).start()

                for k in range(gather_wide):
                    write_out(block + k).start()

            @pl.when(a + s <= last)
            def _():
                block = (a + s) * per_chunk + q * gather_wide
                gather_copy(block, ag_left_send, left_to).wait_recv()

                @pl.when(a > 0)
                def _():
                    gather_copy(block, ag_left_send, left_to).start()

                for k in range(gather_wide):
                    write_out(block + k).start()

        if s == n - 3:
            for j in range(n):
                wait_exchange(j, *totals)
                part = pl.ds(j * rows, rows)
                average = total_in[j].astype(jnp.float32) / n
                moved = MOMENTUM_DECAY * momentum[part, :] + average
                new_momentum[part, :] = moved
                new_outer[part, :] = outer[part, :] - OUTER_RATE * (average + MOMENTUM_DECAY * moved)
            pltpu.make_async_copy(new_outer, new_outer_hbm, out_sem.at[0]).start()
            pltpu.make_async_copy(new_momentum, new_momentum_hbm, out_sem.at[1]).start()

    pltpu.make_async_copy(new_outer, new_outer_hbm, out_sem.at[0]).wait()
    pltpu.make_async_copy(new_momentum, new_momentum_hbm, out_sem.at[1]).wait()
    for j in range(n):
        wait_sent(j, *prior)
        wait_sent(j, *totals)

    def drain(block, carry):
        write_out(block).wait()
        return carry

    lax.fori_loop(0, n * per_chunk, drain, None)

    def drain_sums(piece, carry):
        block = piece * wide
        chunk = piece // PARTS

        @pl.when(chunk > a)
        def _():
            passed_on(from_left, right_send, right_recv, block, right_to).wait_send()

        @pl.when(chunk < a)
        def _():
            passed_on(from_right, left_send, left_recv, block, left_to).wait_send()

        return carry

    lax.fori_loop(0, n * PARTS, drain_sums, None)

    def drain_gather(piece, carry):
        block = piece * gather_wide
        chunk = piece // GATHER_PARTS

        @pl.when((chunk <= a) & (a < last))
        def _():
            gather_copy(block, ag_right_send, right_to).wait_send()

        @pl.when((chunk >= a) & (a > 0))
        def _():
            gather_copy(block, ag_left_send, left_to).wait_send()

        return carry

    lax.fori_loop(0, n * GATHER_PARTS, drain_gather, None)


def solution(mesh):
    n = mesh.shape["rep"]
    finer = Mesh(mesh.devices.reshape(n, n, -1), ("rep", "hi", "lo"))

    def per_device(base_weights, local_weights, outer_params, momentum):
        rows, width = base_weights.shape
        blocks = width // BLOCK
        per_chunk = blocks // n
        bf16, f32 = jnp.bfloat16, jnp.float32
        held = pltpu.VMEM((blocks, rows, BLOCK), bf16)
        eight = pltpu.VMEM((n, rows, BLOCK), bf16)
        owned = outer_params.shape
        dma = pltpu.SemaphoreType.DMA
        anywhere = pl.BlockSpec(memory_space=pl.ANY)
        pieces, gather_pieces = n * PARTS, n * GATHER_PARTS
        return pl.pallas_call(
            functools.partial(kernel, n),
            out_shape=(
                jax.ShapeDtypeStruct(owned, f32),
                jax.ShapeDtypeStruct(owned, f32),
                jax.ShapeDtypeStruct((rows, width), bf16),
            ),
            in_specs=[anywhere] * 4,
            out_specs=(anywhere,) * 3,
            scratch_shapes=[
                pltpu.VMEM((rows, width), bf16), pltpu.VMEM((rows, width), bf16),
                pltpu.VMEM(owned, f32), pltpu.VMEM(owned, f32), pltpu.VMEM(owned, f32), pltpu.VMEM(owned, f32),
                pltpu.VMEM((per_chunk, rows, BLOCK), f32), held, held, held, held,
                eight, eight, eight, eight,
                dma((4,)), dma((2,)), dma((pieces,)), dma((pieces,)), dma((pieces,)), dma((pieces,)),
                dma((n,)), dma((n,)), dma((n,)), dma((n,)),
                dma((gather_pieces,)), dma((gather_pieces,)), dma((gather_pieces,)), dma((blocks,)),
            ],
            compiler_params=pltpu.CompilerParams(collective_id=0, has_side_effects=True),
        )(base_weights, local_weights[0], outer_params, momentum)

    fsdp = ("hi", "lo")
    return jax.shard_map(
        per_device,
        mesh=finer,
        in_specs=(P(fsdp, None), P("rep", fsdp, None), P("rep", fsdp), P("rep", fsdp)),
        out_specs=(P("rep", fsdp), P("rep", fsdp), P(fsdp, None)),
        check_vma=False,
    )
```

```python
import functools

import jax
import jax.numpy as jnp
from jax import lax
from jax.experimental import pallas as pl
from jax.experimental.pallas import tpu as pltpu
from jax.sharding import Mesh
from jax.sharding import PartitionSpec as P

BLOCK = 128
LEVEL_LIMIT = 448.0
EPSILON = 1e-06
OUTER_RATE = 0.7
MOMENTUM_DECAY = 0.9
MESH = pl.DeviceIdType.MESH

FROM_MOMENTUM = OUTER_RATE * MOMENTUM_DECAY * MOMENTUM_DECAY
FROM_AVERAGE = OUTER_RATE * (1.0 + MOMENTUM_DECAY)

PARTS = 4
LAG = 4
GATHER_PARTS = 4


def kernel(n, base_hbm, local_hbm, outer_hbm, momentum_hbm, totals_hbm, weights_hbm,
           base, local, outer, momentum,
           own, sums, from_left, from_right, gathered, prior_out, prior_in, total_out, total_in,
           in_sem, out_sem, right_send, right_recv, left_send, left_recv,
           prior_send, prior_recv, total_send, total_recv, ag_right_send, ag_left_send, ag_recv, weights_sem):
    a, b, l = lax.axis_index("rep"), lax.axis_index("hi"), lax.axis_index("lo")
    last = n - 1
    per_chunk = own.shape[0]
    wide = per_chunk // PARTS
    half = n // 2

    line_half = b // half

    def chunk_of(rank):
        near = line_half * half + rank - 2
        at_start = (1 - line_half) * half + b % 2 + 2 * rank
        at_end = (1 - line_half) * half + 1 - b % 2 + 2 * (rank - (n - 2))
        return jnp.where(rank < 2, at_start, jnp.where(rank >= n - 2, at_end, near))

    mine = chunk_of(a)
    is_near = a // half == b // half
    from_end = b % half // 2
    root = jnp.where(is_near, b % half + 2, jnp.where((a + b) % 2 == 0, from_end, n - 2 + from_end))

    ins = [
        pltpu.make_async_copy(src, dst, in_sem.at[k])
        for k, (src, dst) in enumerate(
            ((outer_hbm, outer), (momentum_hbm, momentum), (base_hbm, base), (local_hbm, local))
        )
    ]
    for copy in ins:
        copy.start()

    barrier = pltpu.get_barrier_semaphore()

    @pl.when(a > 0)
    def _():
        pl.semaphore_signal(barrier, inc=1, device_id={"rep": a - 1}, device_id_type=MESH)

    @pl.when(a < last)
    def _():
        pl.semaphore_signal(barrier, inc=1, device_id={"rep": a + 1}, device_id_type=MESH)

    for j in range(n):
        pl.semaphore_signal(barrier, inc=1, device_id=(root, a, j), device_id_type=MESH)
        pl.semaphore_signal(barrier, inc=1, device_id=(b, mine, j), device_id_type=MESH)

    greeted = 2 * n + 2 - (a == 0).astype(jnp.int32) - (a == last).astype(jnp.int32)

    def prior_copy(j):
        return pltpu.make_async_remote_copy(
            src_ref=prior_out.at[j], dst_ref=prior_in.at[l], send_sem=prior_send.at[j],
            recv_sem=prior_recv.at[l], device_id=(root, a, j), device_id_type=MESH)

    def prior_arrival(j):
        return pltpu.make_async_remote_copy(
            src_ref=prior_out.at[j], dst_ref=prior_in.at[j], send_sem=prior_send.at[j],
            recv_sem=prior_recv.at[j], device_id=(root, a, j), device_id_type=MESH)

    def total_copy(j):
        return pltpu.make_async_remote_copy(
            src_ref=total_out.at[j], dst_ref=total_in.at[l], send_sem=total_send.at[j],
            recv_sem=total_recv.at[l], device_id=(b, mine, j), device_id_type=MESH)

    def total_arrival(j):
        return pltpu.make_async_remote_copy(
            src_ref=total_out.at[j], dst_ref=total_in.at[j], send_sem=total_send.at[j],
            recv_sem=total_recv.at[j], device_id=(b, mine, j), device_id_type=MESH)

    def columns_of(block):
        return pl.ds(pl.multiple_of((chunk_of(block // per_chunk) * per_chunk + block % per_chunk) * BLOCK, BLOCK), BLOCK)

    def dequantized(block):
        columns = columns_of(block)
        pseudo = base[:, columns].astype(jnp.float32) - local[:, columns].astype(jnp.float32)
        largest = jnp.max(jnp.abs(pseudo), axis=1, keepdims=True)
        scale = ((largest + EPSILON) / LEVEL_LIMIT).astype(jnp.bfloat16).astype(jnp.float32)
        levels = (pseudo / scale).astype(jnp.bfloat16).astype(jnp.float32)
        return levels * scale

    ins[0].wait()
    ins[1].wait()
    rows = prior_out.shape[1]
    for j in range(n):
        part = pl.ds(j * rows, rows)
        prior_out[j] = (outer[part, :] - FROM_MOMENTUM * momentum[part, :]).astype(jnp.bfloat16)
    pl.semaphore_wait(barrier, greeted)
    for j in range(n):
        prior_copy(j).start()
    ins[2].wait()
    ins[3].wait()

    def passed_on(arrived, send_sem, recv_sem, block, to):
        return pltpu.make_async_remote_copy(
            src_ref=sums.at[pl.ds(block, wide)], dst_ref=arrived.at[pl.ds(block, wide)],
            send_sem=send_sem.at[block // wide], recv_sem=recv_sem.at[block // wide],
            device_id={"rep": to}, device_id_type=MESH)

    def pass_on(has_input, arrived, send_sem, recv_sem, block, to):
        copy = passed_on(arrived, send_sem, recv_sem, block, to)
        for k in range(wide):
            own[k] = dequantized(block + k)

        @pl.when(has_input)
        def _():
            copy.wait_recv()
            for k in range(wide):
                sums[block + k] = (own[k] + arrived[block + k].astype(jnp.float32)).astype(jnp.bfloat16)

        @pl.when(jnp.logical_not(has_input))
        def _():
            for k in range(wide):
                sums[block + k] = own[k].astype(jnp.bfloat16)

        copy.start()

    def right_block(u):
        return ((last - u // PARTS) * PARTS + u % PARTS) * wide

    def left_block(v):
        return v * wide

    right_to, left_to = jnp.minimum(a + 1, last), jnp.maximum(a - 1, 0)
    right = (from_left, right_send, right_recv)
    left = (from_right, left_send, left_recv)
    right_count, left_count = (last - a) * PARTS, a * PARTS

    def step(t, carry):
        u, v = t - a * LAG, t - (last - a) * LAG

        @pl.when((u >= 0) & (u < right_count))
        def _():
            pass_on(a > 0, *right, right_block(u), right_to)

        @pl.when((v >= 0) & (v < left_count))
        def _():
            pass_on(a < last, *left, left_block(v), left_to)

        return carry

    lax.fori_loop(0, n * max(LAG, PARTS), step, None)

    gather_wide = per_chunk // GATHER_PARTS

    def gather_copy(block, send_sem, to):
        return pltpu.make_async_remote_copy(
            src_ref=gathered.at[pl.ds(block, gather_wide)], dst_ref=gathered.at[pl.ds(block, gather_wide)],
            send_sem=send_sem.at[block // gather_wide], recv_sem=ag_recv.at[block // gather_wide],
            device_id={"rep": to}, device_id_type=MESH)

    def write_out(block):
        return pltpu.make_async_copy(gathered.at[block], weights_hbm.at[:, columns_of(block)], weights_sem.at[block])

    for j in range(n):
        own[j] = dequantized(a * per_chunk + j)
    for q in range(PARTS):
        block = a * per_chunk + q * wide

        @pl.when(a > 0)
        def _():
            passed_on(from_left, right_send, right_recv, block, right_to).wait_recv()
            for k in range(wide):
                own[q * wide + k] += from_left[block + k].astype(jnp.float32)

        @pl.when(a < last)
        def _():
            passed_on(from_right, left_send, left_recv, block, left_to).wait_recv()
            for k in range(wide):
                own[q * wide + k] += from_right[block + k].astype(jnp.float32)

        for k in range(wide):
            j = q * wide + k
            prior_arrival(j).wait_recv()
            total = own[j]
            total_out[j] = total.astype(jnp.bfloat16)
            gathered[block + k] = (
                prior_in[j].astype(jnp.float32) - (FROM_AVERAGE / n) * total).astype(jnp.bfloat16)

        @pl.when(a < last)
        def _():
            gather_copy(block, ag_right_send, right_to).start()

        @pl.when(a > 0)
        def _():
            gather_copy(block, ag_left_send, left_to).start()

        for k in range(wide):
            total_copy(q * wide + k).start()
    for j in range(n):
        write_out(a * per_chunk + j).start()

    def gather_step(t, carry):
        s, q = t // GATHER_PARTS + 1, t % GATHER_PARTS

        @pl.when(s <= a)
        def _():
            block = (a - s) * per_chunk + q * gather_wide
            gather_copy(block, ag_right_send, right_to).wait_recv()

            @pl.when(a < last)
            def _():
                gather_copy(block, ag_right_send, right_to).start()

            for k in range(gather_wide):
                write_out(block + k).start()

        @pl.when(s <= last - a)
        def _():
            block = (a + s) * per_chunk + q * gather_wide
            gather_copy(block, ag_left_send, left_to).wait_recv()

            @pl.when(a > 0)
            def _():
                gather_copy(block, ag_left_send, left_to).start()

            for k in range(gather_wide):
                write_out(block + k).start()

        return carry

    lax.fori_loop(0, last * GATHER_PARTS, gather_step, None)
    for j in range(n):
        total_arrival(j).wait_recv()
        pltpu.make_async_copy(total_in.at[j], totals_hbm.at[j], out_sem.at[j]).start()

    for j in range(n):
        pltpu.make_async_copy(total_in.at[j], totals_hbm.at[j], out_sem.at[j]).wait()
        prior_copy(j).wait_send()
        total_copy(j).wait_send()

    def drain(block, carry):
        write_out(block).wait()
        return carry

    lax.fori_loop(0, n * per_chunk, drain, None)

    def drain_sent(piece, carry):
        block = piece * wide
        rank = piece // PARTS
        above, below = rank > a, rank < a

        @pl.when(above)
        def _():
            passed_on(from_left, right_send, right_recv, block, right_to).wait_send()

        @pl.when(below)
        def _():
            passed_on(from_right, left_send, left_recv, block, left_to).wait_send()

        @pl.when(jnp.logical_not(above) & (a < last))
        def _():
            gather_copy(block, ag_right_send, right_to).wait_send()

        @pl.when(jnp.logical_not(below) & (a > 0))
        def _():
            gather_copy(block, ag_left_send, left_to).wait_send()

        return carry

    lax.fori_loop(0, n * PARTS, drain_sent, None)


def solution(mesh):
    n = mesh.shape["rep"]
    finer = Mesh(mesh.devices.reshape(n, n, -1), ("rep", "hi", "lo"))

    def per_device(base_weights, local_weights, outer_params, momentum):
        rows, width = base_weights.shape
        blocks = width // BLOCK
        per_chunk = blocks // n
        bf16, f32 = jnp.bfloat16, jnp.float32
        held = pltpu.VMEM((blocks, rows, BLOCK), bf16)
        eight = pltpu.VMEM((n, rows, BLOCK), bf16)
        owned = outer_params.shape
        dma = pltpu.SemaphoreType.DMA
        anywhere = pl.BlockSpec(memory_space=pl.ANY)
        pieces, gather_pieces = n * PARTS, n * GATHER_PARTS
        totals, new_weights = pl.pallas_call(
            functools.partial(kernel, n),
            out_shape=(
                jax.ShapeDtypeStruct((n, rows, BLOCK), bf16),
                jax.ShapeDtypeStruct((rows, width), bf16),
            ),
            in_specs=[anywhere] * 4,
            out_specs=(anywhere,) * 2,
            scratch_shapes=[
                pltpu.VMEM((rows, width), bf16), pltpu.VMEM((rows, width), bf16),
                pltpu.VMEM(owned, f32), pltpu.VMEM(owned, f32),
                pltpu.VMEM((per_chunk, rows, BLOCK), f32), held, held, held, held,
                eight, eight, eight, eight,
                dma((4,)), dma((n,)), dma((pieces,)), dma((pieces,)), dma((pieces,)), dma((pieces,)),
                dma((n,)), dma((n,)), dma((n,)), dma((n,)),
                dma((gather_pieces,)), dma((gather_pieces,)), dma((gather_pieces,)), dma((blocks,)),
            ],
            compiler_params=pltpu.CompilerParams(collective_id=0, has_side_effects=True),
        )(base_weights, local_weights[0], outer_params, momentum)
        average = totals.reshape(owned).astype(f32) / n
        new_momentum = MOMENTUM_DECAY * momentum + average
        new_outer = outer_params - OUTER_RATE * (average + MOMENTUM_DECAY * new_momentum)
        return new_outer, new_momentum, new_weights

    fsdp = ("hi", "lo")
    return jax.shard_map(
        per_device,
        mesh=finer,
        in_specs=(P(fsdp, None), P("rep", fsdp, None), P("rep", fsdp), P("rep", fsdp)),
        out_specs=(P("rep", fsdp), P("rep", fsdp), P(fsdp, None)),
        check_vma=False,
    )
```

```python
import functools

import jax
import jax.numpy as jnp
from jax import lax
from jax.experimental import pallas as pl
from jax.experimental.pallas import tpu as pltpu
from jax.sharding import Mesh
from jax.sharding import PartitionSpec as P

BLOCK = 128
LEVEL_LIMIT = 448.0
EPSILON = 1e-06
OUTER_RATE = 0.7
MOMENTUM_DECAY = 0.9
MESH = pl.DeviceIdType.MESH

FROM_MOMENTUM = OUTER_RATE * MOMENTUM_DECAY * MOMENTUM_DECAY
FROM_AVERAGE = OUTER_RATE * (1.0 + MOMENTUM_DECAY)

PARTS = 4
LAG = 5
GATHER_PARTS = 4
ROUND_STEPS = (4, 6, 8, 11, 15, 17)


def kernel(n, base_hbm, local_hbm, outer_hbm, momentum_hbm, averages_hbm, weights_hbm,
           base, local, outer, momentum, average,
           own, sums, from_left, from_right, gathered, prior_out, prior_in, total_out, total_in,
           in_sem, out_sem, right_send, right_recv, left_send, left_recv,
           prior_send, prior_recv, total_send, total_recv, ag_right_send, ag_left_send, ag_recv, weights_sem, known):
    a, b, l = lax.axis_index("rep"), lax.axis_index("hi"), lax.axis_index("lo")
    last = n - 1
    per_chunk = own.shape[0]
    wide = per_chunk // PARTS
    half = n // 2

    line_half = b // half

    def chunk_of(rank):
        near = line_half * half + rank - 2
        at_start = (1 - line_half) * half + b % 2 + 2 * rank
        at_end = (1 - line_half) * half + 1 - b % 2 + 2 * (rank - (n - 2))
        return jnp.where(rank < 2, at_start, jnp.where(rank >= n - 2, at_end, near))

    mine = chunk_of(a)
    is_near = a // half == b // half
    from_end = b % half // 2
    root = jnp.where(is_near, b % half + 2, jnp.where((a + b) % 2 == 0, from_end, n - 2 + from_end))

    ins = [
        pltpu.make_async_copy(src, dst, in_sem.at[k])
        for k, (src, dst) in enumerate(
            ((outer_hbm, outer), (momentum_hbm, momentum), (base_hbm, base), (local_hbm, local))
        )
    ]
    for copy in ins:
        copy.start()

    ring_z, ring_x, ring_y = 2 * n, n // 2, n // 2
    z, x, y, core = b // ring_x * n + a, b % ring_x, l // 2, l % 2

    def at(dz=0, dx=0, dy=0, other=False):
        to_z = (z + dz + ring_z) % ring_z
        return (to_z % n, to_z // n * ring_x + (x + dx) % ring_x,
                (y + dy) % ring_y * 2 + (1 - core if other else core))

    def signal(sem, places):
        for place in places:
            pl.semaphore_signal(sem, inc=1, device_id=place, device_id_type=MESH)

    along_x = [at(dx=d) for d in range(1, ring_x)]
    along_y = [at(dy=d) for d in range(1, ring_y)]
    rounds = [along_x, [at(other=True)]] + [[at(dz=d), at(dz=-d)] for d in (1, 2, 4, 1)]
    greeted = [at(dz=1), at(dz=-1), at(other=True)] + along_x + along_y
    barrier = pltpu.get_barrier_semaphore()
    signal(barrier, greeted)

    def prior_copy(j):
        return pltpu.make_async_remote_copy(
            src_ref=prior_out.at[j], dst_ref=prior_in.at[l], send_sem=prior_send.at[j],
            recv_sem=prior_recv.at[l], device_id=(root, a, j), device_id_type=MESH)

    def prior_arrival(j):
        return pltpu.make_async_remote_copy(
            src_ref=prior_out.at[j], dst_ref=prior_in.at[j], send_sem=prior_send.at[j],
            recv_sem=prior_recv.at[j], device_id=(root, a, j), device_id_type=MESH)

    def total_copy(j):
        return pltpu.make_async_remote_copy(
            src_ref=total_out.at[j], dst_ref=total_in.at[l], send_sem=total_send.at[j],
            recv_sem=total_recv.at[l], device_id=(b, mine, j), device_id_type=MESH)

    def total_arrival(j):
        return pltpu.make_async_remote_copy(
            src_ref=total_out.at[j], dst_ref=total_in.at[j], send_sem=total_send.at[j],
            recv_sem=total_recv.at[j], device_id=(b, mine, j), device_id_type=MESH)

    def columns_of(block):
        return pl.ds(pl.multiple_of((chunk_of(block // per_chunk) * per_chunk + block % per_chunk) * BLOCK, BLOCK), BLOCK)

    def dequantized(block):
        columns = columns_of(block)
        pseudo = base[:, columns].astype(jnp.float32) - local[:, columns].astype(jnp.float32)
        largest = jnp.max(jnp.abs(pseudo), axis=1, keepdims=True)
        scale = ((largest + EPSILON) / LEVEL_LIMIT).astype(jnp.bfloat16).astype(jnp.float32)
        levels = (pseudo / scale).astype(jnp.bfloat16).astype(jnp.float32)
        return levels * scale

    ins[0].wait()
    ins[1].wait()
    rows = prior_out.shape[1]
    for j in range(n):
        part = pl.ds(j * rows, rows)
        prior_out[j] = (outer[part, :] - FROM_MOMENTUM * momentum[part, :]).astype(jnp.bfloat16)
    pl.semaphore_wait(barrier, len(greeted))
    signal(known.at[0], rounds[0])
    ins[2].wait()
    ins[3].wait()

    def passed_on(arrived, send_sem, recv_sem, block, to):
        return pltpu.make_async_remote_copy(
            src_ref=sums.at[pl.ds(block, wide)], dst_ref=arrived.at[pl.ds(block, wide)],
            send_sem=send_sem.at[block // wide], recv_sem=recv_sem.at[block // wide],
            device_id={"rep": to}, device_id_type=MESH)

    def pass_on(has_input, arrived, send_sem, recv_sem, block, to):
        copy = passed_on(arrived, send_sem, recv_sem, block, to)
        for k in range(wide):
            own[k] = dequantized(block + k)

        @pl.when(has_input)
        def _():
            copy.wait_recv()
            for k in range(wide):
                sums[block + k] = (own[k] + arrived[block + k].astype(jnp.float32)).astype(jnp.bfloat16)

        @pl.when(jnp.logical_not(has_input))
        def _():
            for k in range(wide):
                sums[block + k] = own[k].astype(jnp.bfloat16)

        copy.start()

    def right_block(u):
        return ((last - u // PARTS) * PARTS + u % PARTS) * wide

    def left_block(v):
        return v * wide

    right_to, left_to = jnp.minimum(a + 1, last), jnp.maximum(a - 1, 0)
    right = (from_left, right_send, right_recv)
    left = (from_right, left_send, left_recv)
    right_count, left_count = (last - a) * PARTS, a * PARTS

    def step(t, carry):
        u, v = t - a * LAG, t - (last - a) * LAG
        for k in range(len(rounds)):
            @pl.when(t == ROUND_STEPS[k])
            def _():
                pl.semaphore_wait(known.at[k], len(rounds[k]))
                if k + 1 < len(rounds):
                    signal(known.at[k + 1], rounds[k + 1])
                else:
                    for j in range(n):
                        prior_copy(j).start()

        @pl.when((u >= 0) & (u < right_count))
        def _():
            pass_on(a > 0, *right, right_block(u), right_to)

        @pl.when((v >= 0) & (v < left_count))
        def _():
            pass_on(a < last, *left, left_block(v), left_to)

        return carry

    lax.fori_loop(0, n * max(LAG, PARTS), step, None)

    gather_wide = per_chunk // GATHER_PARTS

    def gather_copy(block, send_sem, to):
        return pltpu.make_async_remote_copy(
            src_ref=gathered.at[pl.ds(block, gather_wide)], dst_ref=gathered.at[pl.ds(block, gather_wide)],
            send_sem=send_sem.at[block // gather_wide], recv_sem=ag_recv.at[block // gather_wide],
            device_id={"rep": to}, device_id_type=MESH)

    def write_out(block):
        return pltpu.make_async_copy(gathered.at[block], weights_hbm.at[:, columns_of(block)], weights_sem.at[block])

    for j in range(n):
        own[j] = dequantized(a * per_chunk + j)
    for q in range(PARTS):
        block = a * per_chunk + q * wide

        @pl.when(a > 0)
        def _():
            passed_on(from_left, right_send, right_recv, block, right_to).wait_recv()
            for k in range(wide):
                own[q * wide + k] += from_left[block + k].astype(jnp.float32)

        @pl.when(a < last)
        def _():
            passed_on(from_right, left_send, left_recv, block, left_to).wait_recv()
            for k in range(wide):
                own[q * wide + k] += from_right[block + k].astype(jnp.float32)

        for k in range(wide):
            j = q * wide + k
            prior_arrival(j).wait_recv()
            total = own[j]
            total_out[j] = total.astype(jnp.bfloat16)
            gathered[block + k] = (
                prior_in[j].astype(jnp.float32) - (FROM_AVERAGE / n) * total).astype(jnp.bfloat16)

        @pl.when(a < last)
        def _():
            gather_copy(block, ag_right_send, right_to).start()

        @pl.when(a > 0)
        def _():
            gather_copy(block, ag_left_send, left_to).start()

        for k in range(wide):
            total_copy(q * wide + k).start()
    for j in range(n):
        write_out(a * per_chunk + j).start()

    def passed_sent(rank, q):
        block = rank * per_chunk + q * wide

        @pl.when(rank > a)
        def _():
            passed_on(from_left, right_send, right_recv, block, right_to).wait_send()

        @pl.when(rank < a)
        def _():
            passed_on(from_right, left_send, left_recv, block, left_to).wait_send()

    def gather_sent(s, q):
        @pl.when((s <= a) & (a < last))
        def _():
            gather_copy((a - s) * per_chunk + q * gather_wide, ag_right_send, right_to).wait_send()

        @pl.when((s <= last - a) & (a > 0))
        def _():
            gather_copy((a + s) * per_chunk + q * gather_wide, ag_left_send, left_to).wait_send()

    def gather_written(s, q):
        @pl.when(s <= a)
        def _():
            for k in range(gather_wide):
                write_out((a - s) * per_chunk + q * gather_wide + k).wait()

        @pl.when((s <= last - a) & (s > 0))
        def _():
            for k in range(gather_wide):
                write_out((a + s) * per_chunk + q * gather_wide + k).wait()

    def gather_step(t, carry):
        s, q = t // GATHER_PARTS + 1, t % GATHER_PARTS
        passed_sent(s - 1, q)
        pl.when(s == last)(lambda: passed_sent(s, q))
        pl.when(s >= 3)(lambda: gather_sent(s - 2, q))
        gather_written(s - 1, q)

        @pl.when(s <= a)
        def _():
            block = (a - s) * per_chunk + q * gather_wide
            gather_copy(block, ag_right_send, right_to).wait_recv()

            @pl.when(a < last)
            def _():
                gather_copy(block, ag_right_send, right_to).start()

            for k in range(gather_wide):
                write_out(block + k).start()

        @pl.when(s <= last - a)
        def _():
            block = (a + s) * per_chunk + q * gather_wide
            gather_copy(block, ag_left_send, left_to).wait_recv()

            @pl.when(a > 0)
            def _():
                gather_copy(block, ag_left_send, left_to).start()

            for k in range(gather_wide):
                write_out(block + k).start()

        return carry

    lax.fori_loop(0, last * GATHER_PARTS, gather_step, None)
    for j in range(n):
        total_arrival(j).wait_recv()
        average[pl.ds(j * rows, rows), :] = total_in[j].astype(jnp.float32) / n
    leaving = pltpu.make_async_copy(average, averages_hbm, out_sem.at[0])
    leaving.start()

    for j in range(n):
        prior_copy(j).wait_send()
        total_copy(j).wait_send()
    for q in range(GATHER_PARTS):
        gather_sent(0, q)
        gather_sent(last - 1, q)
        gather_sent(last, q)
        gather_written(last, q)
    leaving.wait()


def solution(mesh):
    n = mesh.shape["rep"]
    finer = Mesh(mesh.devices.reshape(n, n, -1), ("rep", "hi", "lo"))

    def per_device(base_weights, local_weights, outer_params, momentum):
        rows, width = base_weights.shape
        blocks = width // BLOCK
        per_chunk = blocks // n
        bf16, f32 = jnp.bfloat16, jnp.float32
        held = pltpu.VMEM((blocks, rows, BLOCK), bf16)
        eight = pltpu.VMEM((n, rows, BLOCK), bf16)
        owned = outer_params.shape
        dma = pltpu.SemaphoreType.DMA
        anywhere = pl.BlockSpec(memory_space=pl.ANY)
        pieces, gather_pieces = n * PARTS, n * GATHER_PARTS
        average, new_weights = pl.pallas_call(
            functools.partial(kernel, n),
            out_shape=(
                jax.ShapeDtypeStruct(owned, f32),
                jax.ShapeDtypeStruct((rows, width), bf16),
            ),
            in_specs=[anywhere] * 4,
            out_specs=(anywhere,) * 2,
            scratch_shapes=[
                pltpu.VMEM((rows, width), bf16), pltpu.VMEM((rows, width), bf16),
                pltpu.VMEM(owned, f32), pltpu.VMEM(owned, f32), pltpu.VMEM(owned, f32),
                pltpu.VMEM((per_chunk, rows, BLOCK), f32), held, held, held, held,
                eight, eight, eight, eight,
                dma((4,)), dma((n,)), dma((pieces,)), dma((pieces,)), dma((pieces,)), dma((pieces,)),
                dma((n,)), dma((n,)), dma((n,)), dma((n,)),
                dma((gather_pieces,)), dma((gather_pieces,)), dma((gather_pieces,)), dma((blocks,)),
                pltpu.SemaphoreType.REGULAR((6,)),
            ],
            compiler_params=pltpu.CompilerParams(collective_id=0, has_side_effects=True),
        )(base_weights, local_weights[0], outer_params, momentum)
        new_momentum = MOMENTUM_DECAY * momentum + average
        new_outer = outer_params - OUTER_RATE * (average + MOMENTUM_DECAY * new_momentum)
        return new_outer, new_momentum, new_weights

    fsdp = ("hi", "lo")
    return jax.shard_map(
        per_device,
        mesh=finer,
        in_specs=(P(fsdp, None), P("rep", fsdp, None), P("rep", fsdp), P("rep", fsdp)),
        out_specs=(P("rep", fsdp), P("rep", fsdp), P(fsdp, None)),
        check_vma=False,
    )
```

```python
import functools

import jax
import jax.numpy as jnp
from jax import lax
from jax.experimental import pallas as pl
from jax.experimental.pallas import tpu as pltpu
from jax.sharding import Mesh
from jax.sharding import PartitionSpec as P

BLOCK = 128
LEVEL_LIMIT = 448.0
EPSILON = 1e-06
OUTER_RATE = 0.7
MOMENTUM_DECAY = 0.9
MESH = pl.DeviceIdType.MESH

FROM_MOMENTUM = OUTER_RATE * MOMENTUM_DECAY * MOMENTUM_DECAY
FROM_AVERAGE = OUTER_RATE * (1.0 + MOMENTUM_DECAY)

PARTS = 4
LAG = 5
GATHER_PARTS = 4
ROUND_STEPS = (4, 6, 8, 13, 15)


def kernel(n, base_hbm, local_hbm, outer_hbm, momentum_hbm, averages_hbm, weights_hbm,
           base, local, outer, momentum, average,
           own, sums, from_left, from_right, gathered, prior_out, prior_in, total_out, total_in,
           in_sem, out_sem, right_send, right_recv, left_send, left_recv,
           prior_send, prior_recv, total_send, total_recv, ag_right_send, ag_left_send, ag_recv, weights_sem, known):
    a, b, l = lax.axis_index("rep"), lax.axis_index("hi"), lax.axis_index("lo")
    last = n - 1
    per_chunk = own.shape[0]
    wide = per_chunk // PARTS
    half = n // 2

    line_half = b // half

    def chunk_of(rank):
        near = line_half * half + rank - 2
        at_start = (1 - line_half) * half + b % 2 + 2 * rank
        at_end = (1 - line_half) * half + 1 - b % 2 + 2 * (rank - (n - 2))
        return jnp.where(rank < 2, at_start, jnp.where(rank >= n - 2, at_end, near))

    mine = chunk_of(a)
    is_near = a // half == b // half
    from_end = b % half // 2
    root = jnp.where(is_near, b % half + 2, jnp.where((a + b) % 2 == 0, from_end, n - 2 + from_end))

    ins = [
        pltpu.make_async_copy(src, dst, in_sem.at[k])
        for k, (src, dst) in enumerate(
            ((outer_hbm, outer), (momentum_hbm, momentum), (base_hbm, base), (local_hbm, local))
        )
    ]
    for copy in ins:
        copy.start()

    ring_z, ring_x, ring_y = 2 * n, n // 2, n // 2
    z, x, y, core = b // ring_x * n + a, b % ring_x, l // 2, l % 2

    def at(dz=0, dx=0, dy=0, other=False):
        to_z = (z + dz + ring_z) % ring_z
        return (to_z % n, to_z // n * ring_x + (x + dx) % ring_x,
                (y + dy) % ring_y * 2 + (1 - core if other else core))

    def signal(sem, places):
        for place in places:
            pl.semaphore_signal(sem, inc=1, device_id=place, device_id_type=MESH)

    along_x = [at(dx=d) for d in range(1, ring_x)]
    along_y = [at(dy=d) for d in range(1, ring_y)]
    rounds = [along_x, [at(other=True)]] + [[at(dz=d) for d in turn] for turn in ((1, -1, 2, -2), (4, -4), (2, -2))]
    greeted = [at(dz=d) for d in (1, -1, 2, -2)] + [at(other=True)] + along_x + along_y
    barrier = pltpu.get_barrier_semaphore()
    signal(barrier, greeted)

    def prior_copy(j):
        return pltpu.make_async_remote_copy(
            src_ref=prior_out.at[j], dst_ref=prior_in.at[l], send_sem=prior_send.at[j],
            recv_sem=prior_recv.at[l], device_id=(root, a, j), device_id_type=MESH)

    def prior_arrival(j):
        return pltpu.make_async_remote_copy(
            src_ref=prior_out.at[j], dst_ref=prior_in.at[j], send_sem=prior_send.at[j],
            recv_sem=prior_recv.at[j], device_id=(root, a, j), device_id_type=MESH)

    def total_copy(j):
        return pltpu.make_async_remote_copy(
            src_ref=total_out.at[j], dst_ref=total_in.at[l], send_sem=total_send.at[j],
            recv_sem=total_recv.at[l], device_id=(b, mine, j), device_id_type=MESH)

    def total_arrival(j):
        return pltpu.make_async_remote_copy(
            src_ref=total_out.at[j], dst_ref=total_in.at[j], send_sem=total_send.at[j],
            recv_sem=total_recv.at[j], device_id=(b, mine, j), device_id_type=MESH)

    def columns_of(block):
        return pl.ds(pl.multiple_of((chunk_of(block // per_chunk) * per_chunk + block % per_chunk) * BLOCK, BLOCK), BLOCK)

    def dequantized(block):
        columns = columns_of(block)
        pseudo = base[:, columns].astype(jnp.float32) - local[:, columns].astype(jnp.float32)
        largest = jnp.max(jnp.abs(pseudo), axis=1, keepdims=True)
        scale = ((largest + EPSILON) / LEVEL_LIMIT).astype(jnp.bfloat16).astype(jnp.float32)
        levels = (pseudo / scale).astype(jnp.bfloat16).astype(jnp.float32)
        return levels * scale

    ins[0].wait()
    ins[1].wait()
    rows = prior_out.shape[1]
    for j in range(n):
        part = pl.ds(j * rows, rows)
        prior_out[j] = (outer[part, :] - FROM_MOMENTUM * momentum[part, :]).astype(jnp.bfloat16)
    pl.semaphore_wait(barrier, len(greeted))
    signal(known.at[0], rounds[0])
    ins[2].wait()
    ins[3].wait()

    def passed_on(arrived, send_sem, recv_sem, block, to):
        return pltpu.make_async_remote_copy(
            src_ref=sums.at[pl.ds(block, wide)], dst_ref=arrived.at[pl.ds(block, wide)],
            send_sem=send_sem.at[block // wide], recv_sem=recv_sem.at[block // wide],
            device_id={"rep": to}, device_id_type=MESH)

    def pass_on(has_input, arrived, send_sem, recv_sem, block, to):
        copy = passed_on(arrived, send_sem, recv_sem, block, to)
        for k in range(wide):
            own[k] = dequantized(block + k)

        @pl.when(has_input)
        def _():
            copy.wait_recv()
            for k in range(wide):
                sums[block + k] = (own[k] + arrived[block + k].astype(jnp.float32)).astype(jnp.bfloat16)

        @pl.when(jnp.logical_not(has_input))
        def _():
            for k in range(wide):
                sums[block + k] = own[k].astype(jnp.bfloat16)

        copy.start()

    def right_block(u):
        return ((last - u // PARTS) * PARTS + u % PARTS) * wide

    def left_block(v):
        return v * wide

    right_to, left_to = jnp.minimum(a + 1, last), jnp.maximum(a - 1, 0)
    right = (from_left, right_send, right_recv)
    left = (from_right, left_send, left_recv)
    right_count, left_count = (last - a) * PARTS, a * PARTS

    def step(t, carry):
        u, v = t - a * LAG, t - (last - a) * LAG
        for k in range(len(rounds)):
            @pl.when(t == ROUND_STEPS[k])
            def _():
                pl.semaphore_wait(known.at[k], len(rounds[k]))
                if k + 1 < len(rounds):
                    signal(known.at[k + 1], rounds[k + 1])
                else:
                    for j in range(n):
                        prior_copy(j).start()

        @pl.when((u >= 0) & (u < right_count))
        def _():
            pass_on(a > 0, *right, right_block(u), right_to)

        @pl.when((v >= 0) & (v < left_count))
        def _():
            pass_on(a < last, *left, left_block(v), left_to)

        return carry

    lax.fori_loop(0, n * max(LAG, PARTS), step, None)

    gather_wide = per_chunk // GATHER_PARTS

    def gather_copy(block, send_sem, to):
        return pltpu.make_async_remote_copy(
            src_ref=gathered.at[pl.ds(block, gather_wide)], dst_ref=gathered.at[pl.ds(block, gather_wide)],
            send_sem=send_sem.at[block // gather_wide], recv_sem=ag_recv.at[block // gather_wide],
            device_id={"rep": to}, device_id_type=MESH)

    def write_out(block):
        return pltpu.make_async_copy(gathered.at[block], weights_hbm.at[:, columns_of(block)], weights_sem.at[block])

    for j in range(n):
        own[j] = dequantized(a * per_chunk + j)
    for q in range(PARTS):
        block = a * per_chunk + q * wide

        @pl.when(a > 0)
        def _():
            passed_on(from_left, right_send, right_recv, block, right_to).wait_recv()
            for k in range(wide):
                own[q * wide + k] += from_left[block + k].astype(jnp.float32)

        @pl.when(a < last)
        def _():
            passed_on(from_right, left_send, left_recv, block, left_to).wait_recv()
            for k in range(wide):
                own[q * wide + k] += from_right[block + k].astype(jnp.float32)

        for k in range(wide):
            j = q * wide + k
            prior_arrival(j).wait_recv()
            total = own[j]
            total_out[j] = total.astype(jnp.bfloat16)
            gathered[block + k] = (
                prior_in[j].astype(jnp.float32) - (FROM_AVERAGE / n) * total).astype(jnp.bfloat16)

        @pl.when(a < last)
        def _():
            gather_copy(block, ag_right_send, right_to).start()

        @pl.when(a > 0)
        def _():
            gather_copy(block, ag_left_send, left_to).start()

        for k in range(wide):
            total_copy(q * wide + k).start()
    for j in range(n):
        write_out(a * per_chunk + j).start()

    def passed_sent(rank, q):
        block = rank * per_chunk + q * wide

        @pl.when(rank > a)
        def _():
            passed_on(from_left, right_send, right_recv, block, right_to).wait_send()

        @pl.when(rank < a)
        def _():
            passed_on(from_right, left_send, left_recv, block, left_to).wait_send()

    def gather_sent(s, q):
        @pl.when((s <= a) & (a < last))
        def _():
            gather_copy((a - s) * per_chunk + q * gather_wide, ag_right_send, right_to).wait_send()

        @pl.when((s <= last - a) & (a > 0))
        def _():
            gather_copy((a + s) * per_chunk + q * gather_wide, ag_left_send, left_to).wait_send()

    def gather_written(s, q):
        @pl.when(s <= a)
        def _():
            for k in range(gather_wide):
                write_out((a - s) * per_chunk + q * gather_wide + k).wait()

        @pl.when((s <= last - a) & (s > 0))
        def _():
            for k in range(gather_wide):
                write_out((a + s) * per_chunk + q * gather_wide + k).wait()

    def gather_step(t, carry):
        s, q = t // GATHER_PARTS + 1, t % GATHER_PARTS
        passed_sent(s - 1, q)
        pl.when(s == last)(lambda: passed_sent(s, q))
        pl.when(s >= 3)(lambda: gather_sent(s - 2, q))
        gather_written(s - 1, q)

        @pl.when(s <= a)
        def _():
            block = (a - s) * per_chunk + q * gather_wide
            gather_copy(block, ag_right_send, right_to).wait_recv()

            @pl.when(a < last)
            def _():
                gather_copy(block, ag_right_send, right_to).start()

            for k in range(gather_wide):
                write_out(block + k).start()

        @pl.when(s <= last - a)
        def _():
            block = (a + s) * per_chunk + q * gather_wide
            gather_copy(block, ag_left_send, left_to).wait_recv()

            @pl.when(a > 0)
            def _():
                gather_copy(block, ag_left_send, left_to).start()

            for k in range(gather_wide):
                write_out(block + k).start()

        return carry

    lax.fori_loop(0, last * GATHER_PARTS, gather_step, None)
    for j in range(n):
        total_arrival(j).wait_recv()
        average[pl.ds(j * rows, rows), :] = total_in[j].astype(jnp.float32) / n
    leaving = pltpu.make_async_copy(average, averages_hbm, out_sem.at[0])
    leaving.start()

    for j in range(n):
        prior_copy(j).wait_send()
        total_copy(j).wait_send()
    for q in range(GATHER_PARTS):
        gather_sent(0, q)
        gather_sent(last - 1, q)
        gather_sent(last, q)
        gather_written(last, q)
    leaving.wait()


def solution(mesh):
    n = mesh.shape["rep"]
    finer = Mesh(mesh.devices.reshape(n, n, -1), ("rep", "hi", "lo"))

    def per_device(base_weights, local_weights, outer_params, momentum):
        rows, width = base_weights.shape
        blocks = width // BLOCK
        per_chunk = blocks // n
        bf16, f32 = jnp.bfloat16, jnp.float32
        held = pltpu.VMEM((blocks, rows, BLOCK), bf16)
        eight = pltpu.VMEM((n, rows, BLOCK), bf16)
        owned = outer_params.shape
        dma = pltpu.SemaphoreType.DMA
        anywhere = pl.BlockSpec(memory_space=pl.ANY)
        pieces, gather_pieces = n * PARTS, n * GATHER_PARTS
        average, new_weights = pl.pallas_call(
            functools.partial(kernel, n),
            out_shape=(
                jax.ShapeDtypeStruct(owned, f32),
                jax.ShapeDtypeStruct((rows, width), bf16),
            ),
            in_specs=[anywhere] * 4,
            out_specs=(anywhere,) * 2,
            scratch_shapes=[
                pltpu.VMEM((rows, width), bf16), pltpu.VMEM((rows, width), bf16),
                pltpu.VMEM(owned, f32), pltpu.VMEM(owned, f32), pltpu.VMEM(owned, f32),
                pltpu.VMEM((per_chunk, rows, BLOCK), f32), held, held, held, held,
                eight, eight, eight, eight,
                dma((4,)), dma((n,)), dma((pieces,)), dma((pieces,)), dma((pieces,)), dma((pieces,)),
                dma((n,)), dma((n,)), dma((n,)), dma((n,)),
                dma((gather_pieces,)), dma((gather_pieces,)), dma((gather_pieces,)), dma((blocks,)),
                pltpu.SemaphoreType.REGULAR((5,)),
            ],
            compiler_params=pltpu.CompilerParams(collective_id=0, has_side_effects=True),
        )(base_weights, local_weights[0], outer_params, momentum)
        new_momentum = MOMENTUM_DECAY * momentum + average
        new_outer = outer_params - OUTER_RATE * (average + MOMENTUM_DECAY * new_momentum)
        return new_outer, new_momentum, new_weights

    fsdp = ("hi", "lo")
    return jax.shard_map(
        per_device,
        mesh=finer,
        in_specs=(P(fsdp, None), P("rep", fsdp, None), P("rep", fsdp), P("rep", fsdp)),
        out_specs=(P("rep", fsdp), P("rep", fsdp), P(fsdp, None)),
        check_vma=False,
    )
```
